32 devices in a mesh: group: 4 (over y, x), member: 8 (over z, core).
Axes of the slice: x: 2, y: 2, z: 4, core: 2. Of those that a mesh axis runs over, the one named last changes fastest.
Arguments:
- embeddings: float32 [32768, 256], P(('group', 'member')), may hold values from -24 to 24, as said below
- operators: float32 [16, 256, 256], replicated, as said below
- plan: int32 [4], replicated, may hold values from 1 to 31, as said below
- relations: int32 [4, 256], P(None, ('group', 'member')), may hold values from 0 to 15
Outputs:
- new_embeddings: float32 [32768, 256], P(('group', 'member'))
- new_operators: float32 [16, 256, 256], replicated
The draws below stay inside these ranges and needn't reach their ends.
Inputs may be any that keep to these rules, and one draw needn't show every extreme that they name: The 4 values are distinct, so every round pairs distinct partitions two by two; both 1 and 31 occur in every plan. `embeddings`: rows are of order one; some rows may be several times larger. `operators`: each operator is the identity plus a dense full-rank part.
All inputs are finite; a program needn't handle non-finite values.
Results may differ from the reference program's by a relative error of at most 0.015.
The reference program's roundings to bfloat16 on the way count: a program that leaves them out, or rounds other values in their place, can miss the bound.
Values may be sent and summed in bfloat16 or wider, within the bound.
A program may use at most 128 MiB of HBM per device.

```python
import math
import jax
import jax.numpy as jnp
from jax import lax

EMBED_WIDTH = 256
RELS = 16
ROWS = 1024
RB = 128
NEG = 1024
ROUNDS = 4
NODES = 32768
BLOCKS = 256
DEVICES = 32


def draw_embeddings(key, part):
    normal_part = jax.random.normal(jax.random.fold_in(key, 11), (NODES, EMBED_WIDTH), jnp.float32)
    return jnp.clip(normal_part, -6.0, 6.0)


def draw_operators(key, part):
    noise = jax.random.normal(jax.random.fold_in(key, 21), (RELS, EMBED_WIDTH, EMBED_WIDTH), jnp.float32)
    return jnp.eye(EMBED_WIDTH, dtype=jnp.float32)[None, :, :] + 0.6 / jnp.sqrt(jnp.float32(EMBED_WIDTH)) * noise


def draw_plan(key, part):
    middle = jax.random.permutation(jax.random.fold_in(key, 31), DEVICES - 3) + 2
    ends = jnp.array([1, DEVICES - 1], dtype=jnp.int32)
    values = jnp.concatenate([ends, middle[:ROUNDS - 2].astype(jnp.int32)])
    shuffled = jax.random.permutation(jax.random.fold_in(key, 32), values)
    return shuffled.astype(jnp.int32)


def set_ends(entries, key, smallest, largest):
    index_at = [jax.random.randint(jax.random.fold_in(key, axis), (), 0, length) for axis, length in enumerate(entries.shape)]
    widest = entries.shape.index(max(entries.shape))
    neighbour = index_at[:widest] + [(index_at[widest] + 1) % entries.shape[widest]] + index_at[widest + 1:]
    return entries.at[tuple(index_at)].set(smallest).at[tuple(neighbour)].set(largest)


def setup_inputs(seed: int = 0) -> dict:
    streams_of = jax.random.split(jax.random.key(seed), 5)
    return {
        "embeddings": draw_embeddings(jax.random.fold_in(streams_of[4], 71), 0),
        "operators": draw_operators(jax.random.fold_in(streams_of[4], 71), 0),
        "plan": draw_plan(jax.random.fold_in(streams_of[4], 71), 0),
        "relations": set_ends(jax.random.randint(streams_of[3], (ROUNDS, BLOCKS), 0, RELS), jax.random.fold_in(streams_of[3], 1), 0, RELS - 1).astype(jnp.int32),
    }


embed_rate = 1.0
operator_rate = 0.02

def bucket_grads(own_rows, partner, rel_ids, ops_table):
    count_of_rows = own_rows.shape[0]
    block_tiles = rel_ids.shape[0]
    block_rows = count_of_rows // block_tiles
    neg_blocks = count_of_rows // NEG
    scale_of_scores = 1.0 / math.sqrt(EMBED_WIDTH)
    onehot = (rel_ids[:, None] == jnp.arange(RELS, dtype=jnp.int32)[None, :]).astype(jnp.float32)
    picked_rows = jnp.dot(onehot, ops_table, precision=lax.Precision.HIGHEST).astype(jnp.bfloat16).reshape(block_tiles, EMBED_WIDTH, EMBED_WIDTH)
    picked_rows_wide = picked_rows.astype(jnp.float32)
    local_block_tiles = own_rows.reshape(block_tiles, block_rows, EMBED_WIDTH).astype(jnp.float32)
    query_rows = jnp.einsum('rux,rxp->rup', local_block_tiles, picked_rows_wide).astype(jnp.bfloat16)
    query_groupings = query_rows.reshape(neg_blocks, NEG, EMBED_WIDTH).astype(jnp.float32)
    partner_groupings = partner.reshape(neg_blocks, NEG, EMBED_WIDTH).astype(jnp.float32)
    score_matrix = jnp.einsum('mfn,mon->mfo', query_groupings, partner_groupings) * scale_of_scores
    row_prob = jax.nn.softmax(score_matrix, axis=2)
    col_prob = jax.nn.softmax(score_matrix, axis=1)
    identity = jnp.eye(NEG, dtype=jnp.float32)
    score_gradient = ((row_prob - identity + (col_prob - identity)) * scale_of_scores).astype(jnp.bfloat16).astype(jnp.float32)
    query_gradient = jnp.einsum('rti,rie->rte', score_gradient, partner_groupings).astype(jnp.bfloat16)
    right_gradient = jnp.einsum('lfv,lfh->lvh', score_gradient, query_groupings).astype(jnp.bfloat16).reshape(count_of_rows, EMBED_WIDTH)
    query_gradient_blocks = query_gradient.reshape(block_tiles, block_rows, EMBED_WIDTH).astype(jnp.float32)
    left_gradient = jnp.einsum('jts,jus->jtu', query_gradient_blocks, picked_rows_wide).reshape(count_of_rows, EMBED_WIDTH)
    block_gradient = jnp.einsum('vmi,vmg->vig', local_block_tiles, query_gradient_blocks).reshape(block_tiles, EMBED_WIDTH * EMBED_WIDTH)
    op_grad = jnp.dot(onehot.T, block_gradient, precision=lax.Precision.HIGHEST)
    return (left_gradient, right_gradient, op_grad)

def reference(embeddings, operators, plan, relations):
    ops_bf = operators.astype(jnp.bfloat16)
    ops_table = lax.optimization_barrier(ops_bf).astype(jnp.float32).reshape(RELS, EMBED_WIDTH * EMBED_WIDTH)
    embeds = embeddings.reshape(DEVICES, ROWS, EMBED_WIDTH)
    total = jnp.zeros((RELS, EMBED_WIDTH * EMBED_WIDTH), jnp.float32)
    index_list = jnp.arange(DEVICES, dtype=jnp.int32)
    for round_index in range(ROUNDS):
        partner_index = jnp.bitwise_xor(index_list, plan[round_index]).astype(jnp.int32)
        left_rows = embeds.astype(jnp.bfloat16)
        right_rows = left_rows[partner_index]
        rel_rows = relations[round_index].reshape(DEVICES, ROWS // RB)

        def step_one(carry, items):
            left_gradient, right_gradient, op_grad = bucket_grads(items[0], items[1], items[2], ops_table)
            return (carry + op_grad, (left_gradient, right_gradient))
        total, outputs = lax.scan(step_one, total, (left_rows, right_rows, rel_rows))
        left_gradient, right_gradient = outputs
        returned = right_gradient[partner_index].astype(jnp.float32)
        embeds = embeds - embed_rate * (left_gradient + returned)
    new_operators = operators - operator_rate * total.reshape(RELS, EMBED_WIDTH, EMBED_WIDTH)
    return (embeds.reshape(NODES, EMBED_WIDTH), new_operators)
```

```python
import functools
import math

import jax
import jax.numpy as jnp
from jax import lax
from jax.experimental import pallas as pl
from jax.experimental.pallas import tpu as pltpu
from jax.sharding import PartitionSpec as P

AXES = ("group", "member")
embed_rate = 1.0
operator_rate = 0.02
LOG2E = 1.0 / math.log(2.0)
PAD = 16
CHUNK = 128
NT = (((1,), (1,)), ((), ()))
TN = (((0,), (0,)), ((), ()))


def dot(a, b, dims=(((1,), (0,)), ((), ()))):
    return lax.dot_general(a, b, dims, preferred_element_type=jnp.float32)


def softmax_grad(a_ref, b_ref, s_ref, d_ref, emit):
    count, feature = a_ref.shape
    steps = count // CHUNK
    factor = LOG2E / math.sqrt(feature)
    shift = 0.5 * math.log2(feature)
    top = jnp.full((1, count), -jnp.inf, jnp.float32)
    tot = jnp.zeros((1, count), jnp.float32)
    row_lse = []
    for i in range(steps):
        rows = slice(i * CHUNK, (i + 1) * CHUNK)
        s = dot(a_ref[rows, :], b_ref[:count, :], NT) * factor
        s_ref[rows, :] = s
        rmax = jnp.max(s, axis=1, keepdims=True)
        rsum = jnp.sum(jnp.exp2(s - rmax), axis=1, keepdims=True)
        row_lse.append(rmax + jnp.log2(rsum) + shift)
        new = jnp.maximum(top, jnp.max(s, axis=0, keepdims=True))
        tot = tot * jnp.exp2(top - new) + jnp.sum(jnp.exp2(s - new), axis=0, keepdims=True)
        top = new
    col_lse = top + jnp.log2(tot) + shift
    scale = 1.0 / math.sqrt(feature)
    eye = (
        lax.broadcasted_iota(jnp.int32, (CHUNK, CHUNK), 0)
        == lax.broadcasted_iota(jnp.int32, (CHUNK, CHUNK), 1)
    )
    for i in range(steps):
        rows = slice(i * CHUNK, (i + 1) * CHUNK)
        s = s_ref[rows, :]
        d = jnp.exp2(s - row_lse[i]) + jnp.exp2(s - col_lse)
        parts = [d[:, :i * CHUNK]] if i else []
        mid = d[:, i * CHUNK:(i + 1) * CHUNK]
        parts.append(jnp.where(eye, mid - 2.0 * scale, mid))
        if i + 1 < steps:
            parts.append(d[:, (i + 1) * CHUNK:])
        d = jnp.concatenate(parts, axis=1) if len(parts) > 1 else parts[0]
        emit(i, dot(d.astype(jnp.bfloat16), b_ref[:count, :]))


def round_body(
    rel_ref, next_ref, e_ref, own_ref, recv_ref, ops_ref, enew_ref, pay_ref, dq_ref,
    s_ref, d_ref, q_ref, qq_ref,
):
    count, feature = e_ref.shape
    tiles = rel_ref.shape[0]
    rb = count // tiles
    extra = recv_ref[count:, :128].astype(jnp.float32)
    for b in range(tiles):
        rows = slice(b * rb, (b + 1) * rb)
        q_ref[rows, :] = dot(own_ref[rows, :], ops_ref[rel_ref[b]]).astype(jnp.bfloat16)
        other = jnp.max(extra[b:b + 1, :]).astype(jnp.int32)
        qq_ref[rows, :] = dot(recv_ref[rows, :], ops_ref[other]).astype(jnp.bfloat16)

    def emit_left(i, g):
        rows = slice(i * CHUNK, (i + 1) * CHUNK)
        g = g.astype(jnp.bfloat16)
        dq_ref[rows, :] = g
        left = dot(g, ops_ref[rel_ref[i * CHUNK // rb]], NT)
        enew_ref[rows, :] = left

    def emit_right(i, g):
        rows = slice(i * CHUNK, (i + 1) * CHUNK)
        g = g.astype(jnp.bfloat16).astype(jnp.float32)
        new = e_ref[rows, :] - embed_rate * (enew_ref[rows, :] + g)
        enew_ref[rows, :] = new
        pay_ref[rows, :] = new.astype(jnp.bfloat16)

    softmax_grad(q_ref, recv_ref, s_ref, d_ref, emit_left)
    softmax_grad(own_ref, qq_ref, s_ref, d_ref, emit_right)
    index = lax.broadcasted_iota(jnp.int32, (PAD, feature), 0)
    ids = jnp.zeros((PAD, feature), jnp.float32)
    for b in range(tiles):
        ids = jnp.where(index == b, next_ref[b].astype(jnp.float32), ids)
    pay_ref[count:, :] = ids.astype(jnp.bfloat16)


VM = pl.BlockSpec(memory_space=pltpu.VMEM)
SM = pl.BlockSpec(memory_space=pltpu.SMEM)


def run_round(rel, nxt, embeds, own, recv, ops_bf):
    count, feature = embeds.shape
    return pl.pallas_call(
        round_body,
        out_shape=(
            jax.ShapeDtypeStruct((count, feature), jnp.float32),
            jax.ShapeDtypeStruct((count + PAD, feature), jnp.bfloat16),
            jax.ShapeDtypeStruct((count, feature), jnp.bfloat16),
        ),
        in_specs=[SM, SM, VM, VM, VM, VM],
        out_specs=(VM, VM, VM),
        scratch_shapes=[
            pltpu.VMEM((count, count), jnp.float32),
            pltpu.VMEM((CHUNK, count), jnp.bfloat16),
            pltpu.VMEM((count, feature), jnp.bfloat16),
            pltpu.VMEM((count, feature), jnp.bfloat16),
        ],
        name="bucket_round",
    )(rel, nxt, embeds, own, recv, ops_bf)


def grad_body(rel_ref, own_ref, dq_ref, out_ref, g_ref):
    rounds, tiles = rel_ref.shape
    rb = dq_ref.shape[1] // tiles
    g_ref[...] = jnp.zeros_like(g_ref)
    for r in range(rounds):
        for b in range(tiles):
            rows = slice(b * rb, (b + 1) * rb)
            c = rel_ref[r, b]
            g_ref[c] += dot(own_ref[r, rows, :], dq_ref[r, rows, :], TN)
    out_ref[...] = g_ref[...].reshape(out_ref.shape).astype(out_ref.dtype)


def operator_grads(relations, owns, dqs, relation_count):
    feature = dqs.shape[2]
    return pl.pallas_call(
        grad_body,
        out_shape=jax.ShapeDtypeStruct((relation_count * feature, feature), jnp.bfloat16),
        in_specs=[SM, VM, VM],
        out_specs=VM,
        scratch_shapes=[pltpu.VMEM((relation_count, feature, feature), jnp.float32)],
        name="operator_grads",
    )(relations, owns, dqs)


def reduce_body(sizes, orders, in_ref, out_ref, acc_ref, recv_ref, ssem, rsem):
    groups, members = sizes
    me = lax.axis_index("group") * members + lax.axis_index("member")
    nb = (groups * members).bit_length() - 1

    def bit(b):
        return lax.rem(me // (1 << b), 2)

    def partner(b):
        other = me + (1 - 2 * bit(b)) * (1 << b)
        return (other // members, lax.rem(other, members))

    barrier = pltpu.get_barrier_semaphore()
    for b in range(nb):
        pl.semaphore_signal(
            barrier, inc=1, device_id=partner(b), device_id_type=pl.DeviceIdType.MESH
        )
    pl.semaphore_wait(barrier, nb)
    rows = in_ref.shape[0]
    streams = len(orders)
    part = rows // streams
    offs = [jnp.int32(s * part) for s in range(streams)]
    size = part
    base = 0
    for step in range(nb):
        half = size // 2
        copies = []
        src = in_ref if step == 0 else acc_ref
        for s in range(streams):
            b = orders[s][step]
            away = pl.multiple_of(offs[s] + (1 - bit(b)) * half, half)
            copy = pltpu.make_async_remote_copy(
                src_ref=src.at[pl.ds(away, half), :],
                dst_ref=recv_ref.at[pl.ds(s * part + base, half), :],
                send_sem=ssem.at[0, s, step],
                recv_sem=rsem.at[0, s, step],
                device_id=partner(b),
                device_id_type=pl.DeviceIdType.MESH,
            )
            copy.start()
            copies.append(copy)
            offs[s] = pl.multiple_of(offs[s] + bit(b) * half, half)
        for s in range(streams):
            copies[s].wait()
            dst = out_ref if step == nb - 1 else acc_ref
            dst[pl.ds(offs[s], half), :] = (
                src[pl.ds(offs[s], half), :].astype(jnp.float32)
                + recv_ref[pl.ds(s * part + base, half), :].astype(jnp.float32)
            ).astype(jnp.bfloat16)
        base += half
        size = half
    for step in range(nb - 1, -1, -1):
        copies = []
        for s in range(streams):
            b = orders[s][step]
            span = out_ref.at[pl.ds(offs[s], size), :]
            copy = pltpu.make_async_remote_copy(
                src_ref=span,
                dst_ref=span,
                send_sem=ssem.at[1, s, step],
                recv_sem=rsem.at[1, s, step],
                device_id=partner(b),
                device_id_type=pl.DeviceIdType.MESH,
            )
            copy.start()
            copies.append(copy)
            offs[s] = pl.multiple_of(offs[s] - bit(b) * size, size)
        for copy in copies:
            copy.wait()
        size *= 2


def all_sum(values):
    groups, members = lax.axis_size("group"), lax.axis_size("member")
    low = members.bit_length() - 1
    nb = (groups * members).bit_length() - 1
    outer, inner = list(range(low, nb)), list(range(1, low))
    orders = ([0] + outer + inner, [0] + outer[::-1] + inner)
    rows, feature = values.shape
    return pl.pallas_call(
        functools.partial(reduce_body, (groups, members), orders),
        out_shape=jax.ShapeDtypeStruct((rows, feature), jnp.bfloat16),
        in_specs=[VM],
        out_specs=VM,
        scratch_shapes=[
            pltpu.VMEM((rows, feature), jnp.bfloat16),
            pltpu.VMEM((rows, feature), jnp.bfloat16),
            pltpu.SemaphoreType.DMA((2, 2, nb)),
            pltpu.SemaphoreType.DMA((2, 2, nb)),
        ],
        compiler_params=pltpu.CompilerParams(collective_id=0, has_side_effects=True),
        name="all_sum",
    )(values)


def fetch(payload, mask):
    count = lax.axis_size(AXES)

    def direct(m):
        return lambda x: lax.ppermute(x, AXES, [(p, p ^ m) for p in range(count)])

    return lax.switch(mask - 1, [direct(m) for m in range(1, count)], payload)


def shards(embeddings, operators, plan, relations):
    count, feature = embeddings.shape
    relation_count = operators.shape[0]
    rounds, tiles = relations.shape
    ops_bf = operators.astype(jnp.bfloat16)
    ids = jnp.broadcast_to(
        relations[0].astype(jnp.bfloat16)[:, None], (tiles, feature)
    )
    payload = jnp.concatenate(
        [
            embeddings.astype(jnp.bfloat16),
            ids,
            jnp.zeros((PAD - tiles, feature), jnp.bfloat16),
        ]
    )

    def step(carry, xs):
        embeds, pay = carry
        mask, rel, nxt = xs
        recv = fetch(pay, mask)
        embeds, new_pay, dq = run_round(rel, nxt, embeds, pay[:count], recv, ops_bf)
        return (embeds, new_pay), (pay[:count], dq)

    (embeds, _), (owns, dqs) = lax.scan(
        step, (embeddings, payload), (plan, relations, jnp.roll(relations, -1, axis=0))
    )
    partial = operator_grads(relations, owns, dqs, relation_count)
    summed = all_sum(partial).astype(jnp.float32)
    new_operators = operators - operator_rate * summed.reshape(operators.shape)
    return (embeds, new_operators)


def solution(mesh):
    return jax.shard_map(
        shards,
        mesh=mesh,
        in_specs=(P(AXES, None), P(), P(), P(None, AXES)),
        out_specs=(P(AXES, None), P()),
        check_vma=False,
    )
```

```python
import functools
import math

import jax
import jax.numpy as jnp
from jax import lax
from jax.experimental import pallas as pl
from jax.experimental.pallas import tpu as pltpu
from jax.sharding import PartitionSpec as P

AXES = ("group", "member")
embed_rate = 1.0
operator_rate = 0.02
LOG2E = 1.0 / math.log(2.0)
PAD = 16
CHUNK = 128
NT = (((1,), (1,)), ((), ()))
TN = (((0,), (0,)), ((), ()))


def dot(a, b, dims=(((1,), (0,)), ((), ()))):
    return lax.dot_general(a, b, dims, preferred_element_type=jnp.float32)


def softmax_grad(a_ref, b_ref, s_ref, emit):
    count, feature = s_ref.shape[0], a_ref.shape[1]
    steps = count // CHUNK
    factor = LOG2E / math.sqrt(feature)
    shift = 0.5 * math.log2(feature)
    top = jnp.full((1, count), -jnp.inf, jnp.float32)
    tot = jnp.zeros((1, count), jnp.float32)
    row_lse = []
    for i in range(steps):
        rows = slice(i * CHUNK, (i + 1) * CHUNK)
        s = dot(a_ref[rows, :], b_ref[:count, :], NT) * factor
        s_ref[rows, :] = s
        rmax = jnp.max(s, axis=1, keepdims=True)
        rsum = jnp.sum(jnp.exp2(s - rmax), axis=1, keepdims=True)
        row_lse.append(rmax + jnp.log2(rsum) + shift)
        new = jnp.maximum(top, jnp.max(s, axis=0, keepdims=True))
        tot = tot * jnp.exp2(top - new) + jnp.sum(jnp.exp2(s - new), axis=0, keepdims=True)
        top = new
    col_lse = top + jnp.log2(tot) + shift
    scale = 1.0 / math.sqrt(feature)
    eye = (
        lax.broadcasted_iota(jnp.int32, (CHUNK, CHUNK), 0)
        == lax.broadcasted_iota(jnp.int32, (CHUNK, CHUNK), 1)
    )
    for i in range(steps):
        rows = slice(i * CHUNK, (i + 1) * CHUNK)
        s = s_ref[rows, :]
        d = jnp.exp2(s - row_lse[i]) + jnp.exp2(s - col_lse)
        parts = [d[:, :i * CHUNK]] if i else []
        mid = d[:, i * CHUNK:(i + 1) * CHUNK]
        parts.append(jnp.where(eye, mid - 2.0 * scale, mid))
        if i + 1 < steps:
            parts.append(d[:, (i + 1) * CHUNK:])
        d = jnp.concatenate(parts, axis=1) if len(parts) > 1 else parts[0]
        emit(i, dot(d.astype(jnp.bfloat16), b_ref[:count, :]))


def round_body(
    step_ref, rel_ref, e_ref, own_ref, recv_ref, ops_ref, _, __,
    enew_ref, pay_ref, owns_ref, dqs_ref,
    s_ref, q_ref, qq_ref, left_ref, dq_ref, sems,
):
    count, feature = e_ref.shape
    rounds, tiles = rel_ref.shape
    rb = count // tiles
    r = step_ref[0]
    save_own = pltpu.make_async_copy(own_ref.at[:count], owns_ref.at[r], sems.at[0])
    save_own.start()
    extra = recv_ref[count:, :128].astype(jnp.float32)
    for b in range(tiles):
        rows = slice(b * rb, (b + 1) * rb)
        q_ref[rows, :] = dot(own_ref[rows, :], ops_ref[rel_ref[r, b]]).astype(jnp.bfloat16)
        other = jnp.max(extra[b:b + 1, :]).astype(jnp.int32)
        qq_ref[rows, :] = dot(recv_ref[rows, :], ops_ref[other]).astype(jnp.bfloat16)

    def emit_left(i, g):
        rows = slice(i * CHUNK, (i + 1) * CHUNK)
        g = g.astype(jnp.bfloat16)
        dq_ref[rows, :] = g
        left_ref[rows, :] = dot(g, ops_ref[rel_ref[r, i * CHUNK // rb]], NT)

    def emit_right(i, g):
        rows = slice(i * CHUNK, (i + 1) * CHUNK)
        g = g.astype(jnp.bfloat16).astype(jnp.float32)
        new = e_ref[rows, :] - embed_rate * (left_ref[rows, :] + g)
        enew_ref[rows, :] = new
        pay_ref[rows, :] = new.astype(jnp.bfloat16)

    softmax_grad(q_ref, recv_ref, s_ref, emit_left)
    save_dq = pltpu.make_async_copy(dq_ref, dqs_ref.at[r], sems.at[1])
    save_dq.start()
    save_own.wait()
    softmax_grad(own_ref, qq_ref, s_ref, emit_right)
    index = lax.broadcasted_iota(jnp.int32, (PAD, feature), 0)
    ids = jnp.zeros((PAD, feature), jnp.float32)
    nxt = lax.rem(r + 1, rounds)
    for b in range(tiles):
        ids = jnp.where(index == b, rel_ref[nxt, b].astype(jnp.float32), ids)
    pay_ref[count:, :] = ids.astype(jnp.bfloat16)
    save_dq.wait()


VM = pl.BlockSpec(memory_space=pltpu.VMEM)
SM = pl.BlockSpec(memory_space=pltpu.SMEM)
ANY = pl.BlockSpec(memory_space=pl.ANY)


def run_round(step, relations, embeds, own, recv, ops_bf, owns, dqs):
    count, feature = embeds.shape
    like = [jax.ShapeDtypeStruct(x.shape, x.dtype) for x in (embeds, own, owns, dqs)]
    return pl.pallas_call(
        round_body,
        out_shape=tuple(like),
        in_specs=[SM, SM, VM, VM, VM, VM, ANY, ANY],
        out_specs=(VM, VM, ANY, ANY),
        input_output_aliases={2: 0, 3: 1, 6: 2, 7: 3},
        scratch_shapes=[
            pltpu.VMEM((count, count), jnp.float32),
            pltpu.VMEM((count, feature), jnp.bfloat16),
            pltpu.VMEM((count, feature), jnp.bfloat16),
            pltpu.VMEM((count, feature), jnp.float32),
            pltpu.VMEM((count, feature), jnp.bfloat16),
            pltpu.SemaphoreType.DMA((2,)),
        ],
        name="bucket_round",
    )(step, relations, embeds, own, recv, ops_bf, owns, dqs)


def grad_body(rel_ref, own_ref, dq_ref, out_ref, g_ref):
    rounds, tiles = rel_ref.shape
    rb = dq_ref.shape[1] // tiles
    g_ref[...] = jnp.zeros_like(g_ref)
    for r in range(rounds):
        for b in range(tiles):
            rows = slice(b * rb, (b + 1) * rb)
            c = rel_ref[r, b]
            g_ref[c] += dot(own_ref[r, rows, :], dq_ref[r, rows, :], TN)
    out_ref[...] = g_ref[...].reshape(out_ref.shape).astype(out_ref.dtype)


def operator_grads(relations, owns, dqs, relation_count):
    feature = dqs.shape[2]
    return pl.pallas_call(
        grad_body,
        out_shape=jax.ShapeDtypeStruct((relation_count * feature, feature), jnp.bfloat16),
        in_specs=[SM, VM, VM],
        out_specs=VM,
        scratch_shapes=[pltpu.VMEM((relation_count, feature, feature), jnp.float32)],
        name="operator_grads",
    )(relations, owns, dqs)


def reduce_body(sizes, in_ref, out_ref, near_ref, acc_ref, far_ref, ssem, rsem):
    groups, members = sizes
    chips = groups * members // 2
    me = lax.axis_index("group") * members + lax.axis_index("member")
    core, chip = lax.rem(me, 2), me // 2
    half = in_ref.shape[0] // 2
    piece = half // chips

    def ahead(t):
        return lax.rem(chip + t, chips)

    def behind(t):
        return lax.rem(chip + chips - t, chips)

    def at(other_core, other_chip):
        return pl.ds(pl.multiple_of(other_core * half + other_chip * piece, piece), piece)

    def place(other):
        return pl.ds(pl.multiple_of(other * piece, piece), piece)

    def device(other_core, other_chip):
        other = other_chip * 2 + other_core
        return (other // members, lax.rem(other, members))

    def send(phase, t, src, dst, where):
        return pltpu.make_async_remote_copy(
            src_ref=src,
            dst_ref=dst,
            send_sem=ssem.at[phase, t],
            recv_sem=rsem.at[phase, t],
            device_id=where,
            device_id_type=pl.DeviceIdType.MESH,
        )

    sibling = device(1 - core, chip)

    def to_core(t):
        return send(0, t, in_ref.at[at(1 - core, ahead(t))], near_ref.at[place(t)], sibling)

    def to_chip(t):
        return send(1, t, acc_ref.at[place(t)], far_ref.at[place(t)], device(core, ahead(t)))

    def gather(t):
        span = out_ref.at[at(core, chip)]
        return send(2, t, span, span, device(core, ahead(t)))

    def share(t):
        span = out_ref.at[at(core, behind(t))]
        return send(3, t, span, span, sibling)

    def landed(t):
        span = out_ref.at[at(core, behind(t))]
        return send(2, t, span, span, device(core, ahead(t)))

    def shared(t):
        span = out_ref.at[at(1 - core, behind(t))]
        return send(3, t, span, span, sibling)

    def each(low, high, body):
        def one(t, carry):
            body(t)
            return carry

        lax.fori_loop(low, high, one, 0)

    barrier = pltpu.get_barrier_semaphore()

    def greet(where):
        pl.semaphore_signal(
            barrier, inc=1, device_id=where, device_id_type=pl.DeviceIdType.MESH
        )

    greet(sibling)
    each(1, chips, lambda t: greet(device(core, ahead(t))))
    pl.semaphore_wait(barrier, chips)

    def pair_sum(t):
        return in_ref[at(core, ahead(t)), :].astype(jnp.float32) + near_ref[
            place(t), :
        ].astype(jnp.float32)

    each(1, chips, lambda t: to_core(t).start())
    to_core(0).start()

    def combine(t):
        to_core(t).wait_recv()
        acc_ref[place(t), :] = pair_sum(t).astype(jnp.bfloat16)
        to_chip(t).start()

    each(1, chips, combine)
    to_core(0).wait_recv()

    def add(t, total):
        to_chip(t).wait_recv()
        return total + far_ref[place(t), :].astype(jnp.float32)

    total = lax.fori_loop(1, chips, add, pair_sum(0))
    out_ref[at(core, chip), :] = total.astype(jnp.bfloat16)
    each(1, chips, lambda t: gather(t).start())
    share(0).start()

    def forward(t):
        landed(t).wait_recv()
        share(t).start()

    each(1, chips, forward)

    def close(t):
        to_core(t).wait_send()
        share(t).wait_send()
        shared(t).wait_recv()

    each(0, chips, close)

    def close_far(t):
        to_chip(t).wait_send()
        gather(t).wait_send()

    each(1, chips, close_far)


def all_sum(values):
    groups, members = lax.axis_size("group"), lax.axis_size("member")
    chips = groups * members // 2
    rows, feature = values.shape
    buffer = pltpu.VMEM((rows // 2, feature), jnp.bfloat16)
    return pl.pallas_call(
        functools.partial(reduce_body, (groups, members)),
        out_shape=jax.ShapeDtypeStruct((rows, feature), jnp.bfloat16),
        in_specs=[VM],
        out_specs=VM,
        scratch_shapes=[
            buffer,
            buffer,
            buffer,
            pltpu.SemaphoreType.DMA((4, chips)),
            pltpu.SemaphoreType.DMA((4, chips)),
        ],
        compiler_params=pltpu.CompilerParams(collective_id=0, has_side_effects=True),
        name="all_sum",
    )(values)


def fetch(payload, mask):
    count = lax.axis_size(AXES)

    def direct(m):
        return lambda x: lax.ppermute(x, AXES, [(p, p ^ m) for p in range(count)])

    return lax.switch(mask - 1, [direct(m) for m in range(1, count)], payload)


def shards(embeddings, operators, plan, relations):
    count, feature = embeddings.shape
    relation_count = operators.shape[0]
    rounds, tiles = relations.shape
    ops_bf = operators.astype(jnp.bfloat16)
    ids = jnp.broadcast_to(
        relations[0].astype(jnp.bfloat16)[:, None], (tiles, feature)
    )
    payload = jnp.concatenate(
        [
            embeddings.astype(jnp.bfloat16),
            ids,
            jnp.zeros((PAD - tiles, feature), jnp.bfloat16),
        ]
    )

    def step(r, carry):
        embeds, pay, owns, dqs = carry
        recv = fetch(pay, plan[r])
        return run_round(
            jnp.full((1,), r, jnp.int32), relations, embeds, pay, recv, ops_bf, owns, dqs
        )

    stack = jnp.zeros((rounds, count, feature), jnp.bfloat16)
    embeds, _, owns, dqs = lax.fori_loop(
        0, rounds, step, (embeddings, payload, stack, stack)
    )
    partial = operator_grads(relations, owns, dqs, relation_count)
    summed = all_sum(partial).astype(jnp.float32)
    new_operators = operators - operator_rate * summed.reshape(operators.shape)
    return (embeds, new_operators)


def solution(mesh):
    return jax.shard_map(
        shards,
        mesh=mesh,
        in_specs=(P(AXES, None), P(), P(), P(None, AXES)),
        out_specs=(P(AXES, None), P()),
        check_vma=False,
    )
```

```python
import functools
import math

import jax
import jax.numpy as jnp
from jax import lax
from jax.experimental import pallas as pl
from jax.experimental.pallas import tpu as pltpu
from jax.sharding import PartitionSpec as P

AXES = ("group", "member")
embed_rate = 1.0
operator_rate = 0.02
LOG2E = 1.0 / math.log(2.0)
PAD = 16
CHUNK = 128
NT = (((1,), (1,)), ((), ()))
TN = (((0,), (0,)), ((), ()))


def dot(a, b, dims=(((1,), (0,)), ((), ()))):
    return lax.dot_general(a, b, dims, preferred_element_type=jnp.float32)


def softmax_grad(a_ref, b_ref, s_ref, emit):
    count, feature = s_ref.shape[0], a_ref.shape[1]
    steps = count // CHUNK
    factor = LOG2E / math.sqrt(feature)
    shift = 0.5 * math.log2(feature)
    top = jnp.full((1, count), -jnp.inf, jnp.float32)
    tot = jnp.zeros((1, count), jnp.float32)
    row_lse = []
    for i in range(steps):
        rows = slice(i * CHUNK, (i + 1) * CHUNK)
        s = dot(a_ref[rows, :], b_ref[:count, :], NT) * factor
        s_ref[rows, :] = s
        rmax = jnp.max(s, axis=1, keepdims=True)
        rsum = jnp.sum(jnp.exp2(s - rmax), axis=1, keepdims=True)
        row_lse.append(rmax + jnp.log2(rsum) + shift)
        new = jnp.maximum(top, jnp.max(s, axis=0, keepdims=True))
        tot = tot * jnp.exp2(top - new) + jnp.sum(jnp.exp2(s - new), axis=0, keepdims=True)
        top = new
    col_lse = top + jnp.log2(tot) + shift
    scale = 1.0 / math.sqrt(feature)
    eye = (
        lax.broadcasted_iota(jnp.int32, (CHUNK, CHUNK), 0)
        == lax.broadcasted_iota(jnp.int32, (CHUNK, CHUNK), 1)
    )
    for i in range(steps):
        rows = slice(i * CHUNK, (i + 1) * CHUNK)
        s = s_ref[rows, :]
        d = jnp.exp2(s - row_lse[i]) + jnp.exp2(s - col_lse)
        parts = [d[:, :i * CHUNK]] if i else []
        mid = d[:, i * CHUNK:(i + 1) * CHUNK]
        parts.append(jnp.where(eye, mid - 2.0 * scale, mid))
        if i + 1 < steps:
            parts.append(d[:, (i + 1) * CHUNK:])
        d = jnp.concatenate(parts, axis=1) if len(parts) > 1 else parts[0]
        emit(i, dot(d.astype(jnp.bfloat16), b_ref[:count, :]))


def round_body(
    step_ref, rel_ref, e_ref, own_ref, recv_ref, ops_ref, _, __,
    enew_ref, pay_ref, owns_ref, dqs_ref,
    s_ref, q_ref, qq_ref, left_ref, dq_ref, sems,
):
    count, feature = e_ref.shape
    rounds, tiles = rel_ref.shape
    rb = count // tiles
    r = step_ref[0]
    save_own = pltpu.make_async_copy(own_ref.at[:count], owns_ref.at[r], sems.at[0])
    save_own.start()
    extra = recv_ref[count:, :128].astype(jnp.float32)
    for b in range(tiles):
        rows = slice(b * rb, (b + 1) * rb)
        q_ref[rows, :] = dot(own_ref[rows, :], ops_ref[rel_ref[r, b]]).astype(jnp.bfloat16)
        other = jnp.max(extra[b:b + 1, :]).astype(jnp.int32)
        qq_ref[rows, :] = dot(recv_ref[rows, :], ops_ref[other]).astype(jnp.bfloat16)

    def emit_left(i, g):
        rows = slice(i * CHUNK, (i + 1) * CHUNK)
        g = g.astype(jnp.bfloat16)
        dq_ref[rows, :] = g
        left_ref[rows, :] = dot(g, ops_ref[rel_ref[r, i * CHUNK // rb]], NT)

    def emit_right(i, g):
        rows = slice(i * CHUNK, (i + 1) * CHUNK)
        g = g.astype(jnp.bfloat16).astype(jnp.float32)
        new = e_ref[rows, :] - embed_rate * (left_ref[rows, :] + g)
        enew_ref[rows, :] = new
        pay_ref[rows, :] = new.astype(jnp.bfloat16)

    softmax_grad(q_ref, recv_ref, s_ref, emit_left)
    save_dq = pltpu.make_async_copy(dq_ref, dqs_ref.at[r], sems.at[1])
    save_dq.start()
    save_own.wait()
    softmax_grad(own_ref, qq_ref, s_ref, emit_right)
    index = lax.broadcasted_iota(jnp.int32, (PAD, feature), 0)
    ids = jnp.zeros((PAD, feature), jnp.float32)
    nxt = lax.rem(r + 1, rounds)
    for b in range(tiles):
        ids = jnp.where(index == b, rel_ref[nxt, b].astype(jnp.float32), ids)
    pay_ref[count:, :] = ids.astype(jnp.bfloat16)
    save_dq.wait()


VM = pl.BlockSpec(memory_space=pltpu.VMEM)
SM = pl.BlockSpec(memory_space=pltpu.SMEM)
ANY = pl.BlockSpec(memory_space=pl.ANY)


def run_round(step, relations, embeds, own, recv, ops_bf, owns, dqs):
    count, feature = embeds.shape
    like = [jax.ShapeDtypeStruct(x.shape, x.dtype) for x in (embeds, own, owns, dqs)]
    return pl.pallas_call(
        round_body,
        out_shape=tuple(like),
        in_specs=[SM, SM, VM, VM, VM, VM, ANY, ANY],
        out_specs=(VM, VM, ANY, ANY),
        input_output_aliases={2: 0, 3: 1, 6: 2, 7: 3},
        scratch_shapes=[
            pltpu.VMEM((count, count), jnp.float32),
            pltpu.VMEM((count, feature), jnp.bfloat16),
            pltpu.VMEM((count, feature), jnp.bfloat16),
            pltpu.VMEM((count, feature), jnp.float32),
            pltpu.VMEM((count, feature), jnp.bfloat16),
            pltpu.SemaphoreType.DMA((2,)),
        ],
        name="bucket_round",
    )(step, relations, embeds, own, recv, ops_bf, owns, dqs)


def grad_body(rel_ref, own_ref, dq_ref, out_ref, g_ref):
    rounds, tiles = rel_ref.shape
    rb = dq_ref.shape[1] // tiles
    g_ref[...] = jnp.zeros_like(g_ref)
    for r in range(rounds):
        for b in range(tiles):
            rows = slice(b * rb, (b + 1) * rb)
            c = rel_ref[r, b]
            g_ref[c] += dot(own_ref[r, rows, :], dq_ref[r, rows, :], TN)
    out_ref[...] = g_ref[...].reshape(out_ref.shape).astype(out_ref.dtype)


def operator_grads(relations, owns, dqs, relation_count):
    feature = dqs.shape[2]
    return pl.pallas_call(
        grad_body,
        out_shape=jax.ShapeDtypeStruct((relation_count * feature, feature), jnp.bfloat16),
        in_specs=[SM, VM, VM],
        out_specs=VM,
        scratch_shapes=[pltpu.VMEM((relation_count, feature, feature), jnp.float32)],
        name="operator_grads",
    )(relations, owns, dqs)


def reduce_body(sizes, in_ref, out_ref, near_ref, acc_ref, far_ref, mid_ref, end_ref, ssem, rsem):
    groups, members = sizes
    chips = members // 2
    group, member = lax.axis_index("group"), lax.axis_index("member")
    core, chip = lax.rem(member, 2), member // 2
    half = in_ref.shape[0] // 2
    piece = half // (groups * chips)

    def row(t):
        return lax.rem(group + t, groups)

    def row_back(t):
        return lax.rem(group + groups - t, groups)

    def col(u):
        return lax.rem(chip + u, chips)

    def col_back(u):
        return lax.rem(chip + chips - u, chips)

    def at(c, g, m):
        return pl.ds(pl.multiple_of(c * half + (g * chips + m) * piece, piece), piece)

    def slot(t, u):
        return pl.ds(pl.multiple_of((t * chips + u) * piece, piece), piece)

    def send(phase, k, src, dst, where):
        return pltpu.make_async_remote_copy(
            src_ref=src,
            dst_ref=dst,
            send_sem=ssem.at[phase, k],
            recv_sem=rsem.at[phase, k],
            device_id=where,
            device_id_type=pl.DeviceIdType.MESH,
        )

    sibling = (group, chip * 2 + 1 - core)

    def over_group(t):
        return (row(t), member)

    def over_member(u):
        return (group, col(u) * 2 + core)

    def key(t, u):
        return t * chips + u

    def core_in(t, u):
        return send(
            0, key(t, u), in_ref.at[at(1 - core, row(t), col(u))], near_ref.at[slot(t, u)], sibling
        )

    def group_in(t, u):
        return send(1, key(t, u), acc_ref.at[slot(t, u)], far_ref.at[slot(t, u)], over_group(t))

    def member_in(u):
        return send(2, u, mid_ref.at[slot(0, u)], end_ref.at[slot(0, u)], over_member(u))

    def member_out(u):
        span = out_ref.at[at(core, group, chip)]
        return send(3, u, span, span, over_member(u))

    def member_got(u):
        span = out_ref.at[at(core, group, col_back(u))]
        return send(3, u, span, span, over_member(u))

    def group_out(t, u):
        span = out_ref.at[at(core, group, col_back(u))]
        return send(4, key(t, u), span, span, over_group(t))

    def group_got(t, u):
        span = out_ref.at[at(core, row_back(t), col_back(u))]
        return send(4, key(t, u), span, span, over_group(t))

    def core_out(t, u):
        span = out_ref.at[at(core, row_back(t), col_back(u))]
        return send(5, key(t, u), span, span, sibling)

    def core_got(t, u):
        span = out_ref.at[at(1 - core, row_back(t), col_back(u))]
        return send(5, key(t, u), span, span, sibling)

    def each(low, high, body):
        def one(t, carry):
            body(t)
            return carry

        lax.fori_loop(low, high, one, 0)

    def peers(u, body):
        each(1, groups, lambda t: body(t, u))

    barrier = pltpu.get_barrier_semaphore()

    def greet(where):
        pl.semaphore_signal(
            barrier, inc=1, device_id=where, device_id_type=pl.DeviceIdType.MESH
        )

    greet(sibling)
    each(1, groups, lambda t: greet(over_group(t)))
    each(1, chips, lambda u: greet(over_member(u)))
    pl.semaphore_wait(barrier, groups + chips - 1)

    def pair_sum(t, u):
        return in_ref[at(core, row(t), col(u)), :].astype(jnp.float32) + near_ref[
            slot(t, u), :
        ].astype(jnp.float32)

    def start_core(i):
        u = chips - 1 - i
        peers(u, lambda t, u: core_in(t, u).start())
        core_in(0, u).start()

    each(0, chips, start_core)

    def start_group(i):
        u = chips - 1 - i

        def one(t, u):
            core_in(t, u).wait_recv()
            acc_ref[slot(t, u), :] = pair_sum(t, u).astype(jnp.bfloat16)
            group_in(t, u).start()

        peers(u, one)
        core_in(0, u).wait_recv()

    each(0, chips, start_group)

    def group_sum(u):
        def add(t, total):
            group_in(t, u).wait_recv()
            return total + far_ref[slot(t, u), :].astype(jnp.float32)

        return lax.fori_loop(1, groups, add, pair_sum(0, u))

    def start_member(i):
        u = chips - 1 - i
        mid_ref[slot(0, u), :] = group_sum(u).astype(jnp.bfloat16)
        member_in(u).start()

    each(0, chips - 1, start_member)

    def add_member(i, total):
        u = chips - 1 - i
        member_in(u).wait_recv()
        return total + end_ref[slot(0, u), :].astype(jnp.float32)

    total = lax.fori_loop(0, chips - 1, add_member, group_sum(0))
    out_ref[at(core, group, chip), :] = total.astype(jnp.bfloat16)
    each(1, chips, lambda u: member_out(u).start())
    peers(0, lambda t, u: group_out(t, u).start())
    core_out(0, 0).start()

    def spread(u):
        member_got(u).wait_recv()
        peers(u, lambda t, u: group_out(t, u).start())
        core_out(0, u).start()

    each(1, chips, spread)

    def relay(u):
        def one(t, u):
            group_got(t, u).wait_recv()
            core_out(t, u).start()

        peers(u, one)

    each(0, chips, relay)

    def close(u):
        def one(t, u):
            group_in(t, u).wait_send()
            group_out(t, u).wait_send()

        peers(u, one)

        def pair(t):
            core_in(t, u).wait_send()
            core_out(t, u).wait_send()
            core_got(t, u).wait_recv()

        each(0, groups, pair)

    each(0, chips, close)

    def close_member(u):
        member_in(u).wait_send()
        member_out(u).wait_send()

    each(1, chips, close_member)


def all_sum(values):
    groups, members = lax.axis_size("group"), lax.axis_size("member")
    rows, feature = values.shape
    count = groups * members // 2
    buffer = pltpu.VMEM((rows // 2, feature), jnp.bfloat16)
    small = pltpu.VMEM((rows // 2 // groups, feature), jnp.bfloat16)
    return pl.pallas_call(
        functools.partial(reduce_body, (groups, members)),
        out_shape=jax.ShapeDtypeStruct((rows, feature), jnp.bfloat16),
        in_specs=[VM],
        out_specs=VM,
        scratch_shapes=[
            buffer,
            buffer,
            buffer,
            small,
            small,
            pltpu.SemaphoreType.DMA((6, count)),
            pltpu.SemaphoreType.DMA((6, count)),
        ],
        compiler_params=pltpu.CompilerParams(collective_id=0, has_side_effects=True),
        name="all_sum",
    )(values)


def fetch(payload, mask):
    count = lax.axis_size(AXES)

    def direct(m):
        return lambda x: lax.ppermute(x, AXES, [(p, p ^ m) for p in range(count)])

    return lax.switch(mask - 1, [direct(m) for m in range(1, count)], payload)


def shards(embeddings, operators, plan, relations):
    count, feature = embeddings.shape
    relation_count = operators.shape[0]
    rounds, tiles = relations.shape
    ops_bf = operators.astype(jnp.bfloat16)
    ids = jnp.broadcast_to(
        relations[0].astype(jnp.bfloat16)[:, None], (tiles, feature)
    )
    payload = jnp.concatenate(
        [
            embeddings.astype(jnp.bfloat16),
            ids,
            jnp.zeros((PAD - tiles, feature), jnp.bfloat16),
        ]
    )

    def step(r, carry):
        embeds, pay, owns, dqs = carry
        recv = fetch(pay, plan[r])
        return run_round(
            jnp.full((1,), r, jnp.int32), relations, embeds, pay, recv, ops_bf, owns, dqs
        )

    stack = jnp.zeros((rounds, count, feature), jnp.bfloat16)
    embeds, _, owns, dqs = lax.fori_loop(
        0, rounds, step, (embeddings, payload, stack, stack)
    )
    partial = operator_grads(relations, owns, dqs, relation_count)
    summed = all_sum(partial).reshape(operators.shape)
    new_operators = operators - operator_rate * summed.astype(jnp.float32)
    return (embeds, new_operators)


def solution(mesh):
    return jax.shard_map(
        shards,
        mesh=mesh,
        in_specs=(P(AXES, None), P(), P(), P(None, AXES)),
        out_specs=(P(AXES, None), P()),
        check_vma=False,
    )
```

```python
import functools
import math

import jax
import jax.numpy as jnp
from jax import lax
from jax.experimental import pallas as pl
from jax.experimental.pallas import tpu as pltpu
from jax.sharding import PartitionSpec as P

AXES = ("group", "member")
embed_rate = 1.0
operator_rate = 0.02
LOG2E = 1.0 / math.log(2.0)
PAD = 16
CHUNK = 128
NT = (((1,), (1,)), ((), ()))
TN = (((0,), (0,)), ((), ()))


def dot(a, b, dims=(((1,), (0,)), ((), ()))):
    return lax.dot_general(a, b, dims, preferred_element_type=jnp.float32)


def softmax_grad(a_ref, b_ref, s_ref, emit):
    count, feature = s_ref.shape[0], a_ref.shape[1]
    steps = count // CHUNK
    factor = LOG2E / math.sqrt(feature)
    shift = 0.5 * math.log2(feature)
    top = jnp.full((1, count), -jnp.inf, jnp.float32)
    tot = jnp.zeros((1, count), jnp.float32)
    row_lse = []
    for i in range(steps):
        rows = slice(i * CHUNK, (i + 1) * CHUNK)
        s = dot(a_ref[rows, :], b_ref[:count, :], NT) * factor
        s_ref[rows, :] = s
        rmax = jnp.max(s, axis=1, keepdims=True)
        rsum = jnp.sum(jnp.exp2(s - rmax), axis=1, keepdims=True)
        row_lse.append(rmax + jnp.log2(rsum) + shift)
        new = jnp.maximum(top, jnp.max(s, axis=0, keepdims=True))
        tot = tot * jnp.exp2(top - new) + jnp.sum(jnp.exp2(s - new), axis=0, keepdims=True)
        top = new
    col_lse = top + jnp.log2(tot) + shift
    scale = 1.0 / math.sqrt(feature)
    eye = (
        lax.broadcasted_iota(jnp.int32, (CHUNK, CHUNK), 0)
        == lax.broadcasted_iota(jnp.int32, (CHUNK, CHUNK), 1)
    )
    for i in range(steps):
        rows = slice(i * CHUNK, (i + 1) * CHUNK)
        s = s_ref[rows, :]
        d = jnp.exp2(s - row_lse[i]) + jnp.exp2(s - col_lse)
        parts = [d[:, :i * CHUNK]] if i else []
        mid = d[:, i * CHUNK:(i + 1) * CHUNK]
        parts.append(jnp.where(eye, mid - 2.0 * scale, mid))
        if i + 1 < steps:
            parts.append(d[:, (i + 1) * CHUNK:])
        d = jnp.concatenate(parts, axis=1) if len(parts) > 1 else parts[0]
        emit(i, dot(d.astype(jnp.bfloat16), b_ref[:count, :]))


def round_body(
    step_ref, rel_ref, e_ref, own_ref, recv_ref, ops_ref, _, __,
    enew_ref, pay_ref, owns_ref, dqs_ref,
    s_ref, q_ref, qq_ref, left_ref, dq_ref, sems,
):
    count, feature = e_ref.shape
    rounds, tiles = rel_ref.shape
    rb = count // tiles
    r = step_ref[0]
    save_own = pltpu.make_async_copy(own_ref.at[:count], owns_ref.at[r], sems.at[0])
    save_own.start()
    extra = recv_ref[count:, :128].astype(jnp.float32)
    for b in range(tiles):
        rows = slice(b * rb, (b + 1) * rb)
        q_ref[rows, :] = dot(own_ref[rows, :], ops_ref[rel_ref[r, b]]).astype(jnp.bfloat16)
        other = jnp.max(extra[b:b + 1, :]).astype(jnp.int32)
        qq_ref[rows, :] = dot(recv_ref[rows, :], ops_ref[other]).astype(jnp.bfloat16)

    def emit_left(i, g):
        rows = slice(i * CHUNK, (i + 1) * CHUNK)
        g = g.astype(jnp.bfloat16)
        dq_ref[rows, :] = g
        left_ref[rows, :] = dot(g, ops_ref[rel_ref[r, i * CHUNK // rb]], NT)

    def emit_right(i, g):
        rows = slice(i * CHUNK, (i + 1) * CHUNK)
        g = g.astype(jnp.bfloat16).astype(jnp.float32)
        new = e_ref[rows, :] - embed_rate * (left_ref[rows, :] + g)
        enew_ref[rows, :] = new
        pay_ref[rows, :] = new.astype(jnp.bfloat16)

    softmax_grad(q_ref, recv_ref, s_ref, emit_left)
    save_dq = pltpu.make_async_copy(dq_ref, dqs_ref.at[r], sems.at[1])
    save_dq.start()
    save_own.wait()
    softmax_grad(own_ref, qq_ref, s_ref, emit_right)
    index = lax.broadcasted_iota(jnp.int32, (PAD, feature), 0)
    ids = jnp.zeros((PAD, feature), jnp.float32)
    nxt = lax.rem(r + 1, rounds)
    for b in range(tiles):
        ids = jnp.where(index == b, rel_ref[nxt, b].astype(jnp.float32), ids)
    pay_ref[count:, :] = ids.astype(jnp.bfloat16)
    save_dq.wait()


VM = pl.BlockSpec(memory_space=pltpu.VMEM)
SM = pl.BlockSpec(memory_space=pltpu.SMEM)
ANY = pl.BlockSpec(memory_space=pl.ANY)


def run_round(step, relations, embeds, own, recv, ops_bf, owns, dqs):
    count, feature = embeds.shape
    like = [jax.ShapeDtypeStruct(x.shape, x.dtype) for x in (embeds, own, owns, dqs)]
    return pl.pallas_call(
        round_body,
        out_shape=tuple(like),
        in_specs=[SM, SM, VM, VM, VM, VM, ANY, ANY],
        out_specs=(VM, VM, ANY, ANY),
        input_output_aliases={2: 0, 3: 1, 6: 2, 7: 3},
        scratch_shapes=[
            pltpu.VMEM((count, count), jnp.float32),
            pltpu.VMEM((count, feature), jnp.bfloat16),
            pltpu.VMEM((count, feature), jnp.bfloat16),
            pltpu.VMEM((count, feature), jnp.float32),
            pltpu.VMEM((count, feature), jnp.bfloat16),
            pltpu.SemaphoreType.DMA((2,)),
        ],
        name="bucket_round",
    )(step, relations, embeds, own, recv, ops_bf, owns, dqs)


def grad_body(rel_ref, own_ref, dq_ref, out_ref, g_ref):
    rounds, tiles = rel_ref.shape
    rb = dq_ref.shape[1] // tiles
    g_ref[...] = jnp.zeros_like(g_ref)
    for r in range(rounds):
        for b in range(tiles):
            rows = slice(b * rb, (b + 1) * rb)
            c = rel_ref[r, b]
            g_ref[c] += dot(own_ref[r, rows, :], dq_ref[r, rows, :], TN)
    out_ref[...] = g_ref[...].reshape(out_ref.shape).astype(out_ref.dtype)


def operator_grads(relations, owns, dqs, relation_count):
    feature = dqs.shape[2]
    return pl.pallas_call(
        grad_body,
        out_shape=jax.ShapeDtypeStruct((relation_count * feature, feature), jnp.bfloat16),
        in_specs=[SM, VM, VM],
        out_specs=VM,
        scratch_shapes=[pltpu.VMEM((relation_count, feature, feature), jnp.float32)],
        name="operator_grads",
    )(relations, owns, dqs)


def reduce_body(sizes, in_ref, out_ref, near_ref, acc_ref, far_ref, mid_ref, end_ref, ssem, rsem):
    groups, members = sizes
    chips = members // 2
    group, member = lax.axis_index("group"), lax.axis_index("member")
    core, chip = lax.rem(member, 2), member // 2
    half = in_ref.shape[0] // 2
    piece = half // (groups * chips)

    def row(t):
        return lax.rem(group + t, groups)

    def row_back(t):
        return lax.rem(group + groups - t, groups)

    def col(u):
        return lax.rem(chip + u, chips)

    def col_back(u):
        return lax.rem(chip + chips - u, chips)

    def at(c, g, m):
        return pl.ds(pl.multiple_of(c * half + (g * chips + m) * piece, piece), piece)

    def slot(t, u):
        return pl.ds(pl.multiple_of((t * chips + u) * piece, piece), piece)

    def send(phase, k, src, dst, where):
        return pltpu.make_async_remote_copy(
            src_ref=src,
            dst_ref=dst,
            send_sem=ssem.at[phase, k],
            recv_sem=rsem.at[phase, k],
            device_id=where,
            device_id_type=pl.DeviceIdType.MESH,
        )

    sibling = (group, chip * 2 + 1 - core)

    def over_group(t):
        return (row(t), member)

    def over_member(u):
        return (group, col(u) * 2 + core)

    def key(t, u):
        return t * chips + u

    def core_in(t, u):
        return send(
            0, key(t, u), in_ref.at[at(1 - core, row(t), col(u))], near_ref.at[slot(t, u)], sibling
        )

    def group_in(t, u):
        return send(1, key(t, u), acc_ref.at[slot(t, u)], far_ref.at[slot(t, u)], over_group(t))

    def member_in(u):
        return send(2, u, mid_ref.at[slot(0, u)], end_ref.at[slot(0, u)], over_member(u))

    def member_out(u):
        span = out_ref.at[at(core, group, chip)]
        return send(3, u, span, span, over_member(u))

    def member_got(u):
        span = out_ref.at[at(core, group, col_back(u))]
        return send(3, u, span, span, over_member(u))

    def group_out(t, u):
        span = out_ref.at[at(core, group, col_back(u))]
        return send(4, key(t, u), span, span, over_group(t))

    def group_got(t, u):
        span = out_ref.at[at(core, row_back(t), col_back(u))]
        return send(4, key(t, u), span, span, over_group(t))

    def core_out(t, u):
        span = out_ref.at[at(core, row_back(t), col_back(u))]
        return send(5, key(t, u), span, span, sibling)

    def core_got(t, u):
        span = out_ref.at[at(1 - core, row_back(t), col_back(u))]
        return send(5, key(t, u), span, span, sibling)

    def each(low, high, body):
        def one(t, carry):
            body(t)
            return carry

        lax.fori_loop(low, high, one, 0)

    def peers(u, body):
        each(1, groups, lambda t: body(t, u))

    barrier = pltpu.get_barrier_semaphore()

    def greet(where):
        pl.semaphore_signal(
            barrier, inc=1, device_id=where, device_id_type=pl.DeviceIdType.MESH
        )

    greet(sibling)
    each(1, groups, lambda t: greet(over_group(t)))
    each(1, chips, lambda u: greet(over_member(u)))
    pl.semaphore_wait(barrier, groups + chips - 1)

    def pair_sum(t, u):
        return in_ref[at(core, row(t), col(u)), :].astype(jnp.float32) + near_ref[
            slot(t, u), :
        ].astype(jnp.float32)

    def start_core(i):
        u = chips - 1 - i
        peers(u, lambda t, u: core_in(t, u).start())
        core_in(0, u).start()

    each(0, chips, start_core)

    def start_group(i):
        u = chips - 1 - i

        def one(t, u):
            core_in(t, u).wait_recv()
            acc_ref[slot(t, u), :] = pair_sum(t, u).astype(jnp.bfloat16)
            group_in(t, u).start()

        peers(u, one)
        core_in(0, u).wait_recv()

    each(0, chips, start_group)

    def group_sum(u):
        def add(t, total):
            group_in(t, u).wait_recv()
            return total + far_ref[slot(t, u), :].astype(jnp.float32)

        return lax.fori_loop(1, groups, add, pair_sum(0, u))

    def start_member(i):
        u = chips - 1 - i
        mid_ref[slot(0, u), :] = group_sum(u).astype(jnp.bfloat16)
        member_in(u).start()

    each(0, chips - 1, start_member)

    def add_member(i, total):
        u = chips - 1 - i
        member_in(u).wait_recv()
        return total + end_ref[slot(0, u), :].astype(jnp.float32)

    total = lax.fori_loop(0, chips - 1, add_member, group_sum(0))
    out_ref[at(core, group, chip), :] = total.astype(jnp.bfloat16)
    each(1, chips, lambda u: member_out(u).start())
    peers(0, lambda t, u: group_out(t, u).start())
    core_out(0, 0).start()

    def spread(u):
        member_got(u).wait_recv()
        peers(u, lambda t, u: group_out(t, u).start())
        core_out(0, u).start()

    each(1, chips, spread)

    def relay(u):
        def one(t, u):
            group_got(t, u).wait_recv()
            core_out(t, u).start()

        peers(u, one)

    each(0, chips, relay)

    def close(u):
        def one(t, u):
            group_in(t, u).wait_send()
            group_out(t, u).wait_send()

        peers(u, one)

        def pair(t):
            core_in(t, u).wait_send()
            core_out(t, u).wait_send()
            core_got(t, u).wait_recv()

        each(0, groups, pair)

    each(0, chips, close)

    def close_member(u):
        member_in(u).wait_send()
        member_out(u).wait_send()

    each(1, chips, close_member)


def all_sum(values):
    groups, members = lax.axis_size("group"), lax.axis_size("member")
    rows, feature = values.shape
    count = groups * members // 2
    buffer = pltpu.VMEM((rows // 2, feature), jnp.bfloat16)
    small = pltpu.VMEM((rows // 2 // groups, feature), jnp.bfloat16)
    return pl.pallas_call(
        functools.partial(reduce_body, (groups, members)),
        out_shape=jax.ShapeDtypeStruct((rows, feature), jnp.bfloat16),
        in_specs=[VM],
        out_specs=VM,
        scratch_shapes=[
            buffer,
            buffer,
            buffer,
            small,
            small,
            pltpu.SemaphoreType.DMA((6, count)),
            pltpu.SemaphoreType.DMA((6, count)),
        ],
        compiler_params=pltpu.CompilerParams(collective_id=0, has_side_effects=True),
        name="all_sum",
    )(values)


def update_body(old_ref, sum_ref, new_ref):
    new_ref[...] = old_ref[...] - operator_rate * sum_ref[...].astype(jnp.float32)


def update_operators(operators, summed):
    relation_count, feature, _ = operators.shape
    block = pl.BlockSpec((2, feature, feature), lambda i: (i, 0, 0))
    return pl.pallas_call(
        update_body,
        grid=(relation_count // 2,),
        out_shape=jax.ShapeDtypeStruct(operators.shape, jnp.float32),
        in_specs=[block, block],
        out_specs=block,
        name="update_operators",
    )(operators, summed)


def fetch(payload, mask):
    count = lax.axis_size(AXES)

    def direct(m):
        return lambda x: lax.ppermute(x, AXES, [(p, p ^ m) for p in range(count)])

    return lax.switch(mask - 1, [direct(m) for m in range(1, count)], payload)


def shards(embeddings, operators, plan, relations):
    count, feature = embeddings.shape
    relation_count = operators.shape[0]
    rounds, tiles = relations.shape
    ops_bf = operators.astype(jnp.bfloat16)
    ids = jnp.broadcast_to(
        relations[0].astype(jnp.bfloat16)[:, None], (tiles, feature)
    )
    payload = jnp.concatenate(
        [
            embeddings.astype(jnp.bfloat16),
            ids,
            jnp.zeros((PAD - tiles, feature), jnp.bfloat16),
        ]
    )

    def step(r, carry):
        embeds, pay, owns, dqs = carry
        recv = fetch(pay, plan[r])
        return run_round(
            jnp.full((1,), r, jnp.int32), relations, embeds, pay, recv, ops_bf, owns, dqs
        )

    stack = jnp.zeros((rounds, count, feature), jnp.bfloat16)
    embeds, _, owns, dqs = lax.fori_loop(
        0, rounds, step, (embeddings, payload, stack, stack)
    )
    partial = operator_grads(relations, owns, dqs, relation_count)
    new_operators = update_operators(operators, all_sum(partial).reshape(operators.shape))
    return (embeds, new_operators)


def solution(mesh):
    return jax.shard_map(
        shards,
        mesh=mesh,
        in_specs=(P(AXES, None), P(), P(), P(None, AXES)),
        out_specs=(P(AXES, None), P()),
        check_vma=False,
    )
```
